128 devices in a mesh: expert: 32 (over z, x, core), replica: 4 (over y).
Axes of the slice: x: 4, y: 4, z: 4, core: 2. Of those that a mesh axis runs over, the one named last changes fastest.
Arguments:
- atom_rows: bfloat16 [16384, 512], P(('expert', 'replica')), may hold values from -6 to 6
- grad_out: bfloat16 [16384, 512], P(('expert', 'replica')), may hold values from -6 to 6
- expert_ids: int32 [16384, 1], P(('expert', 'replica')), may hold values from 0 to 31; in each aligned block of 128 rows (0 to 127, 128 to 255, ...) at most 8 rows name the same one
- weight_in: bfloat16 [32, 512, 4096], P('expert', None, 'replica'), may hold values from -0.25 to 0.25
- weight_out: bfloat16 [32, 4096, 512], P('expert', 'replica'), may hold values from -0.09375 to 0.09375
Outputs:
- grad_atoms: bfloat16 [16384, 512], P(('expert', 'replica'))
- grad_weight_in: float32 [32, 512, 4096], P('expert', None, 'replica')
- grad_weight_out: float32 [32, 4096, 512], P('expert', 'replica')
The draws below stay inside these ranges and needn't reach their ends.
Inputs may be any that keep to these rules, and one draw needn't show every extreme that they name: `expert_ids`: in each aligned block of 128 rows (the rows of one device) no expert is named by more than 8 rows, and in some block one expert is named by exactly 8 rows; every expert is named somewhere.
All inputs are finite; a program needn't handle non-finite values.
Results may differ from the reference program's by a relative error of at most 0.0049.
Values may be sent and summed in bfloat16 or wider, within the bound.
No kernel may reach another device: no remote copies, remote signals or barrier semaphores. Data moves between devices by JAX's collectives and lax.ppermute only.
A program may use at most 64 MiB of HBM per device.

```python
import math
import jax
import jax.numpy as jnp
import numpy as np
from jax import lax

D = 512
FF = 4096
ROWS_DEV = 128
EXPERTS = 32
CAP = 8
TOKENS = 16384
N_EXPERT = 32
N_REPLICA = 4


def shard_levels(stream_key, dims, shards, low, high):
    gain, own = 1.0, jax.random.fold_in(stream_key, 6)
    for axis_at, shards_of in shards:
        heights = jnp.exp(jax.random.uniform(jax.random.fold_in(own, axis_at), (shards_of,), jnp.float32, low / len(shards), high / len(shards)))
        gain = gain * jnp.repeat(heights, dims[axis_at] // shards_of).reshape([-1 if axis == axis_at else 1 for axis in range(len(dims))])
    return gain


def assign_block(own_key, own, number, rows, number_of, top, most, skew):
    order = jax.random.permutation(own_key, number_of)
    packed, usual = portions_of(number_of, rows * top, most, skew, True), portions_of(number_of, rows * top, most, skew, False)
    places = jnp.arange(number_of)

    def named(sizes, rotation):
        used = int((sizes > 0).sum())
        fixed = max(1, used // 4)
        passed = fixed + (places - fixed + rotation * (used - fixed)) % max(1, number_of - fixed)
        return jnp.zeros((number_of,), jnp.int32).at[order[jnp.where(places < fixed, places, passed)]].set(jnp.asarray(sizes, jnp.int32))

    sizes = jnp.where(number % 4 == 0, named(packed, number // 4), named(usual, number - number // 4 - 1))
    mixed = jax.random.permutation(jax.random.fold_in(own, 3), number_of)
    source_of, receiver = mixed[0:number_of // 2 * 2:2], mixed[1:number_of // 2 * 2:2]
    margin = jnp.minimum(sizes[source_of] - 1, most - sizes[receiver]) // 2
    margin = jnp.where((source_of == order[0]) | (receiver == order[0]) | (sizes[receiver] == 0), 0, jnp.maximum(margin, 0))
    passed = jax.random.randint(jax.random.fold_in(own, 4), (number_of // 2,), 0, 1 << 20) % (margin + 1)
    sizes = sizes.at[source_of].add(-passed).at[receiver].add(passed)
    items = jnp.searchsorted(jnp.cumsum(sizes), jnp.arange(rows * top), side="right").astype(jnp.int32)
    table = items.reshape(top, rows).T
    table = table[jax.random.permutation(jax.random.fold_in(own, 1), rows)]
    rotation = jax.random.randint(jax.random.fold_in(own, 2), (rows, 1), 0, top)
    return jnp.take_along_axis(table, (jnp.arange(top)[None, :] + rotation) % top, axis=1)


def portions_of(amount, total, bound, lean, full):
    loads = [(1 << 20) // math.isqrt(rank ** lean) + 1 for rank in range(1, amount + 1)]
    largest = bound if full else min(bound, max(-(-total // amount), total * loads[0] // sum(loads)))
    least = 1 if total - largest >= amount - 1 else 0
    holding, spare = [largest] + [least] * (amount - 1), total - largest - least * (amount - 1)
    while spare > 0:
        movable = [i for i in range(1, amount) if holding[i] < largest] or [i for i in range(1, amount) if holding[i] < bound]
        whole, remaining = sum([loads[i] for i in movable]), spare
        for i in movable:
            more = min(bound - holding[i], max(1, remaining * loads[i] // whole), spare)
            holding[i] = holding[i] + more
            spare = spare - more
    return np.array(holding)


def gaussian(own_key, shape, scale, limit, shards=(), kind=jnp.bfloat16):
    values = scale * jax.random.normal(own_key, shape, jnp.float32)
    if shards:
        values = values * shard_levels(own_key, shape, shards, -0.22, 0.18)
    return jnp.clip(values, -limit, limit).astype(kind)


def setup_inputs(seed: int = 0) -> dict:
    arg_keys = jax.random.split(jax.random.key(seed), 6)
    atom_rows = gaussian(arg_keys[0], (TOKENS, D), 1.0, 6.0, ((0, 128),))
    grad_out = gaussian(arg_keys[1], (TOKENS, D), 1.0, 6.0, ((0, 128),))
    expert_ids_keys = jax.random.split(jax.random.fold_in(arg_keys[2], 1), TOKENS // ROWS_DEV)
    expert_ids_turns = jax.random.permutation(jax.random.fold_in(arg_keys[2], 3), TOKENS // ROWS_DEV)
    expert_ids = jax.vmap(lambda own, number: assign_block(jax.random.fold_in(arg_keys[2], 2), own, number, ROWS_DEV, EXPERTS, 1, CAP, 2))(expert_ids_keys, expert_ids_turns).reshape((TOKENS, 1))
    weight_in = gaussian(arg_keys[3], (EXPERTS, D, FF), D ** -0.5, 0.25, ((0, 32), (2, 4)))
    weight_out = gaussian(arg_keys[4], (EXPERTS, FF, D), FF ** -0.5, 0.09375, ((0, 32), (1, 4)))
    return dict(atom_rows=atom_rows, grad_out=grad_out, expert_ids=expert_ids, weight_in=weight_in, weight_out=weight_out)


def expert_backward(rows_in, rows_grad, weight_first, weight_second):
    preact = jnp.dot(rows_in, weight_first, preferred_element_type=jnp.float32)
    gate_sig = jax.nn.sigmoid(preact)
    activation = (preact * gate_sig).astype(jnp.bfloat16)
    grad_act = lax.dot_general(rows_grad, weight_second, (((1,), (1,)), ((), ())), preferred_element_type=jnp.float32)
    grad_pre = (grad_act * gate_sig * (1.0 + preact * (1.0 - gate_sig))).astype(jnp.bfloat16)
    grad_first = lax.dot_general(rows_in, grad_pre, (((0,), (0,)), ((), ())), preferred_element_type=jnp.float32)
    grad_second = lax.dot_general(activation, rows_grad, (((0,), (0,)), ((), ())), preferred_element_type=jnp.float32)
    partial_value = lax.dot_general(grad_pre, weight_first, (((1,), (1,)), ((), ())), preferred_element_type=jnp.float32)
    return grad_first, grad_second, partial_value


def reference(atom_rows, grad_out, expert_ids, weight_in, weight_out):
    labels = expert_ids[:, 0].astype(jnp.int32)
    row_count = labels.shape[0]
    sorted_rows = jnp.argsort(labels, stable=True).astype(jnp.int32)
    onehot = (labels[:, None] == jnp.arange(EXPERTS, dtype=jnp.int32)[None, :]).astype(jnp.int32)
    counts = jnp.sum(onehot, axis=0).astype(jnp.int32)
    starts = (jnp.cumsum(counts) - counts).astype(jnp.int32)
    max_rows = N_EXPERT * N_REPLICA * CAP
    padded = jnp.concatenate([sorted_rows, jnp.zeros((max_rows,), jnp.int32)])

    def per_expert(expert):
        row_index = lax.dynamic_slice_in_dim(padded, starts[expert].astype(jnp.int32), max_rows).astype(jnp.int32)
        live_rows = jnp.arange(max_rows, dtype=jnp.int32) < counts[expert]
        rows_in = jnp.where(live_rows[:, None], atom_rows[row_index], jnp.zeros((), atom_rows.dtype))
        rows_grad = jnp.where(live_rows[:, None], grad_out[row_index], jnp.zeros((), grad_out.dtype))
        grad_first, grad_second, partial_value = expert_backward(rows_in, rows_grad, weight_in[expert], weight_out[expert])
        partial_value = jnp.where(live_rows[:, None], partial_value, jnp.zeros((), partial_value.dtype))
        return grad_first, grad_second, partial_value, row_index

    grad_first, grad_second, partials, indices = lax.map(per_expert, jnp.arange(EXPERTS, dtype=jnp.int32))
    width = atom_rows.shape[1]
    grad_rows = jnp.zeros((row_count, width), partials.dtype).at[indices.reshape(-1)].add(partials.reshape(-1, width))
    return grad_rows.astype(jnp.bfloat16), grad_first, grad_second
```

```python
import functools

import jax
import jax.numpy as jnp
from jax import lax
from jax.experimental import pallas as pl
from jax.experimental.pallas import tpu as pltpu
from jax.sharding import PartitionSpec as P

VMEM = pltpu.VMEM


def slots_of(labels, experts, capacity):
    rows = labels.shape[1]
    named = lax.broadcasted_iota(jnp.int32, (experts, rows), 0) == labels
    earlier = lax.broadcasted_iota(jnp.int32, (rows, rows), 0) < lax.broadcasted_iota(jnp.int32, (rows, rows), 1)
    before = jnp.dot(
        named.astype(jnp.float32).astype(jnp.bfloat16),
        earlier.astype(jnp.float32).astype(jnp.bfloat16),
        preferred_element_type=jnp.float32,
    )
    place = jnp.sum(jnp.where(named, before, 0.0), axis=0, keepdims=True)
    return labels * capacity + place.astype(jnp.int32)


def slot_table(slots, count):
    table = lax.broadcasted_iota(jnp.int32, (count, slots.shape[1]), 0) == slots
    return table.astype(jnp.float32).astype(jnp.bfloat16)


def pack_kernel(experts, replicas, capacity, ids_ref, rows_ref, grad_ref, out_ref):
    table = slot_table(slots_of(ids_ref[...], experts, capacity), experts * capacity)
    width = rows_ref.shape[1]
    for at, ref in ((0, rows_ref), (width, grad_ref)):
        packed = jnp.dot(table, ref[...], preferred_element_type=jnp.float32).astype(jnp.bfloat16)
        packed = packed.reshape(experts, capacity, width)
        for replica in range(replicas):
            out_ref[:, replica, :, at : at + width] = packed


def pack(ids, rows, grad, experts, replicas, capacity):
    return pl.pallas_call(
        functools.partial(pack_kernel, experts, replicas, capacity),
        out_shape=jax.ShapeDtypeStruct((experts, replicas, capacity, 2 * rows.shape[1]), jnp.bfloat16),
        in_specs=[pl.BlockSpec(memory_space=VMEM)] * 3,
        out_specs=pl.BlockSpec(memory_space=VMEM),
        name="pack",
    )(ids, rows, grad)


def unpack_kernel(experts, replicas, capacity, ids_ref, parts_ref, out_ref):
    table = slot_table(slots_of(ids_ref[...], experts, capacity), experts * capacity)
    total = parts_ref[:, 0].astype(jnp.float32)
    for replica in range(1, replicas):
        total = total + parts_ref[:, replica].astype(jnp.float32)
    total = total.astype(jnp.bfloat16).reshape(experts * capacity, out_ref.shape[1])
    out_ref[...] = lax.dot_general(
        table, total, (((0,), (0,)), ((), ())), preferred_element_type=jnp.float32
    ).astype(jnp.bfloat16)


def unpack(ids, parts, experts, replicas, capacity):
    return pl.pallas_call(
        functools.partial(unpack_kernel, experts, replicas, capacity),
        out_shape=jax.ShapeDtypeStruct((ids.shape[1], parts.shape[-1]), jnp.bfloat16),
        in_specs=[pl.BlockSpec(memory_space=VMEM)] * 2,
        out_specs=pl.BlockSpec(memory_space=VMEM),
        name="unpack",
    )(ids, parts)


def expert_backward(rows_in, rows_grad, weight_first, weight_second):
    preact = jnp.dot(rows_in, weight_first, preferred_element_type=jnp.float32)
    gate_sig = jax.nn.sigmoid(preact)
    activation = (preact * gate_sig).astype(jnp.bfloat16)
    grad_act = lax.dot_general(
        rows_grad, weight_second, (((1,), (1,)), ((), ())), preferred_element_type=jnp.float32
    )
    grad_pre = (grad_act * gate_sig * (1.0 + preact * (1.0 - gate_sig))).astype(jnp.bfloat16)
    partial_value = lax.dot_general(
        grad_pre, weight_first, (((1,), (1,)), ((), ())), preferred_element_type=jnp.float32
    ).astype(jnp.bfloat16)
    grad_first = lax.dot_general(
        rows_in, grad_pre, (((0,), (0,)), ((), ())), preferred_element_type=jnp.float32
    )
    grad_second = lax.dot_general(
        activation, rows_grad, (((0,), (0,)), ((), ())), preferred_element_type=jnp.float32
    )
    return (grad_first, grad_second, partial_value)


def body(atom_rows, grad_out, expert_ids, weight_in, weight_out):
    experts = lax.axis_size("expert")
    replicas = lax.axis_size("replica")
    local_rows = atom_rows.shape[0]
    width = atom_rows.shape[1]
    capacity = 2 * local_rows // experts
    ids = expert_ids.reshape(1, local_rows)
    copies = pack(ids, atom_rows, grad_out, experts, replicas, capacity)
    copies = copies.reshape(experts * replicas, capacity, 2 * width)
    arrived = lax.all_to_all(copies, ("expert", "replica"), split_axis=0, concat_axis=0, tiled=True)
    arrived = arrived.reshape(experts * replicas * capacity, 2 * width)
    grad_first, grad_second, partial_value = expert_backward(
        arrived[:, :width], arrived[:, width:], weight_in[0], weight_out[0]
    )
    returned = lax.all_to_all(
        partial_value.reshape(experts * replicas, capacity, width),
        ("expert", "replica"),
        split_axis=0,
        concat_axis=0,
        tiled=True,
    )
    grad_rows = unpack(ids, returned.reshape(experts, replicas, capacity, width), experts, replicas, capacity)
    return (grad_rows, grad_first[None], grad_second[None])


def solution(mesh):
    return jax.shard_map(
        body,
        mesh=mesh,
        in_specs=(
            P(("expert", "replica"), None),
            P(("expert", "replica"), None),
            P(("expert", "replica"), None),
            P("expert", None, "replica"),
            P("expert", "replica", None),
        ),
        out_specs=(
            P(("expert", "replica"), None),
            P("expert", None, "replica"),
            P("expert", "replica", None),
        ),
        check_vma=False,
    )
```

```python
import functools

import jax
import jax.numpy as jnp
from jax import lax
from jax.experimental import pallas as pl
from jax.experimental.pallas import tpu as pltpu
from jax.sharding import PartitionSpec as P

VMEM = pl.BlockSpec(memory_space=pltpu.VMEM)
SMEM = pl.BlockSpec(memory_space=pltpu.SMEM)
BF16 = jnp.bfloat16
F32 = jnp.float32


def limit(mib):
    return pltpu.CompilerParams(vmem_limit_bytes=mib << 20)


def slots_of(labels, experts, capacity):
    rows = labels.shape[1]
    named = lax.broadcasted_iota(jnp.int32, (experts, rows), 0) == labels
    earlier = lax.broadcasted_iota(jnp.int32, (rows, rows), 0) < lax.broadcasted_iota(jnp.int32, (rows, rows), 1)
    before = jnp.dot(named.astype(F32).astype(BF16), earlier.astype(F32).astype(BF16), preferred_element_type=F32)
    place = jnp.sum(jnp.where(named, before, 0.0), axis=0, keepdims=True)
    return labels * capacity + place.astype(jnp.int32)


def slot_table(slots, count):
    table = lax.broadcasted_iota(jnp.int32, (count, slots.shape[1]), 0) == slots
    return table.astype(F32).astype(BF16)


def pack_kernel(experts, capacity, ids_ref, rows_ref, grad_ref, out_ref):
    table = slot_table(slots_of(ids_ref[...], experts, capacity), experts * capacity)
    width = rows_ref.shape[1]
    for at, ref in ((0, rows_ref), (width, grad_ref)):
        out_ref[:, at : at + width] = jnp.dot(table, ref[...], preferred_element_type=F32).astype(BF16)


def pack(ids, rows, grad, experts, capacity):
    return pl.pallas_call(
        functools.partial(pack_kernel, experts, capacity),
        out_shape=jax.ShapeDtypeStruct((experts * capacity, 2 * rows.shape[1]), BF16),
        in_specs=[VMEM] * 3,
        out_specs=VMEM,
        compiler_params=limit(8),
        name="pack",
    )(ids, rows, grad)


def unpack_kernel(experts, replicas, capacity, ids_ref, parts_ref, out_ref):
    table = slot_table(slots_of(ids_ref[...], experts, capacity), experts * capacity)
    total = parts_ref[:, 0].astype(F32)
    for replica in range(1, replicas):
        total = total + parts_ref[:, replica].astype(F32)
    total = total.astype(BF16).reshape(experts * capacity, out_ref.shape[1])
    out_ref[...] = lax.dot_general(
        table, total, (((0,), (0,)), ((), ())), preferred_element_type=F32
    ).astype(BF16)


def unpack(ids, parts, experts, replicas, capacity):
    return pl.pallas_call(
        functools.partial(unpack_kernel, experts, replicas, capacity),
        out_shape=jax.ShapeDtypeStruct((ids.shape[1], parts.shape[-1]), BF16),
        in_specs=[VMEM] * 2,
        out_specs=VMEM,
        compiler_params=limit(8),
        name="unpack",
    )(ids, parts)


def group_math(first_ref, second_ref, win_ref, wout_ref, act_ref, pre_ref, store):
    width = win_ref.shape[0]
    hidden = win_ref.shape[1]
    tile = 256
    both = jnp.concatenate([first_ref[...], second_ref[...]], axis=0)
    rows_in, rows_grad = both[:, :width], both[:, width:]
    total = None
    for at in range(0, hidden, tile):
        win = win_ref[:, at : at + tile]
        preact = jnp.dot(rows_in, win, preferred_element_type=F32)
        grad_act = lax.dot_general(
            rows_grad, wout_ref[at : at + tile, :], (((1,), (1,)), ((), ())), preferred_element_type=F32
        )
        gate_sig = jax.nn.sigmoid(preact)
        act_ref[:, at : at + tile] = (preact * gate_sig).astype(BF16)
        grad_pre = (grad_act * gate_sig * (1.0 + preact * (1.0 - gate_sig))).astype(BF16)
        pre_ref[:, at : at + tile] = grad_pre
        part = lax.dot_general(grad_pre, win, (((1,), (1,)), ((), ())), preferred_element_type=F32)
        total = part if total is None else total + part
    store(total.astype(BF16))


def group_kernel(first_ref, second_ref, win_ref, wout_ref, act_ref, pre_ref, part_ref):
    def store(value):
        part_ref[...] = value

    group_math(first_ref, second_ref, win_ref, wout_ref, act_ref, pre_ref, store)


def last_kernel(capacity, replicas, where_ref, first_ref, second_ref, win_ref, wout_ref, own_ref, near_ref, late_ref,
                act_ref, pre_ref, out_ref):
    sources, width = out_ref.shape[0], out_ref.shape[3]
    cut = sources // 2
    place = [lax.rem(where_ref[0] + k, replicas) for k in range(replicas)]

    def put(value, low, high):
        value = value.reshape(sources, capacity, width)
        out_ref[:cut, pl.ds(low, 1)] = value[:cut].reshape(cut, 1, capacity, width)
        out_ref[cut:, pl.ds(high, 1)] = value[cut:].reshape(sources - cut, 1, capacity, width)

    put(own_ref[...], place[0], place[0])
    put(near_ref[...], place[3], place[1])
    put(late_ref[...], place[1], place[3])
    group_math(first_ref, second_ref, win_ref, wout_ref, act_ref, pre_ref, lambda value: put(value, place[2], place[2]))


def cost(rows, width, hidden):
    return pl.CostEstimate(
        flops=6 * rows * width * hidden, bytes_accessed=4 * width * hidden, transcendentals=rows * hidden
    )


def group(first, second, win, wout):
    rows = first.shape[0] + second.shape[0]
    width, hidden = win.shape
    return pl.pallas_call(
        group_kernel,
        out_shape=(
            jax.ShapeDtypeStruct((rows, hidden), BF16),
            jax.ShapeDtypeStruct((rows, hidden), BF16),
            jax.ShapeDtypeStruct((rows, width), BF16),
        ),
        in_specs=[VMEM] * 4,
        out_specs=(VMEM,) * 3,
        compiler_params=limit(16),
        cost_estimate=cost(rows, width, hidden),
        name="group",
    )(first, second, win, wout)


def last_group(where, first, second, win, wout, own, near, late, experts, replicas, capacity):
    rows = first.shape[0] + second.shape[0]
    width, hidden = win.shape
    return pl.pallas_call(
        functools.partial(last_kernel, capacity, replicas),
        out_shape=(
            jax.ShapeDtypeStruct((rows, hidden), BF16),
            jax.ShapeDtypeStruct((rows, hidden), BF16),
            jax.ShapeDtypeStruct((experts, replicas, capacity, width), BF16),
        ),
        in_specs=[SMEM] + [VMEM] * 7,
        out_specs=(VMEM,) * 3,
        compiler_params=limit(16),
        cost_estimate=cost(rows, width, hidden),
        name="last_group",
    )(where, first, second, win, wout, own, near, late)


def body(atom_rows, grad_out, expert_ids, weight_in, weight_out):
    experts = lax.axis_size("expert")
    replicas = lax.axis_size("replica")
    local_rows = atom_rows.shape[0]
    width = atom_rows.shape[1]
    capacity = 2 * local_rows // experts
    win, wout = weight_in[0], weight_out[0]
    ids = expert_ids.reshape(1, local_rows)
    where = lax.axis_index("replica").astype(jnp.int32).reshape(1)
    packed = pack(ids, atom_rows, grad_out, experts, capacity)
    own = lax.all_to_all(
        packed.reshape(experts, capacity, 2 * width), "expert", split_axis=0, concat_axis=0, tiled=True
    ).reshape(experts * capacity, 2 * width)
    up = [(i, (i + 1) % replicas) for i in range(replicas)]
    down = [(i, (i - 1) % replicas) for i in range(replicas)]
    half = experts * capacity // 2
    low, high = own[:half], own[half:]
    below_low = lax.ppermute(low, "replica", up)
    above_high = lax.ppermute(high, "replica", down)
    below_high = lax.ppermute(high, "replica", up)
    above_low = lax.ppermute(low, "replica", down)
    far_low = lax.ppermute(below_low, "replica", up)
    far_high = lax.ppermute(above_high, "replica", down)
    act0, pre0, part0 = group(low, high, win, wout)
    act1, pre1, part1 = group(below_low, above_high, win, wout)
    act2, pre2, part2 = group(above_low, below_high, win, wout)
    act3, pre3, sending = last_group(
        where, far_low, far_high, win, wout, part0, part1, part2, experts, replicas, capacity
    )
    returned = lax.all_to_all(
        sending.reshape(experts * replicas, capacity, width),
        ("expert", "replica"),
        split_axis=0,
        concat_axis=0,
        tiled=True,
    )
    rows = jnp.concatenate([own, below_low, above_high, above_low, below_high, far_low, far_high], axis=0)
    act = jnp.concatenate([act0, act1, act2, act3], axis=0)
    pre = jnp.concatenate([pre0, pre1, pre2, pre3], axis=0)
    over_rows = (((0,), (0,)), ((), ()))
    grad_first = lax.dot_general(rows[:, :width], pre, over_rows, preferred_element_type=F32)
    grad_second = lax.dot_general(act, rows[:, width:], over_rows, preferred_element_type=F32)
    grad_rows = unpack(ids, returned.reshape(experts, replicas, capacity, width), experts, replicas, capacity)
    return (grad_rows, grad_first[None], grad_second[None])


def solution(mesh):
    return jax.shard_map(
        body,
        mesh=mesh,
        in_specs=(
            P(("expert", "replica"), None),
            P(("expert", "replica"), None),
            P(("expert", "replica"), None),
            P("expert", None, "replica"),
            P("expert", "replica", None),
        ),
        out_specs=(
            P(("expert", "replica"), None),
            P("expert", None, "replica"),
            P("expert", "replica", None),
        ),
        check_vma=False,
    )
```

```python
import functools

import jax
import jax.numpy as jnp
from jax import lax
from jax.experimental import pallas as pl
from jax.experimental.pallas import tpu as pltpu
from jax.sharding import PartitionSpec as P


VMEM = pl.BlockSpec(memory_space=pltpu.VMEM)
SMEM = pl.BlockSpec(memory_space=pltpu.SMEM)
HBM = pl.BlockSpec(memory_space=pltpu.HBM)
DMA = pltpu.SemaphoreType.DMA
BF16 = jnp.bfloat16
F32 = jnp.float32


def limit(mib):
    return pltpu.CompilerParams(vmem_limit_bytes=mib << 20)


def slots_of(labels, experts, capacity):
    rows = labels.shape[1]
    named = lax.broadcasted_iota(jnp.int32, (experts, rows), 0) == labels
    earlier = lax.broadcasted_iota(jnp.int32, (rows, rows), 0) < lax.broadcasted_iota(jnp.int32, (rows, rows), 1)
    before = jnp.dot(named.astype(F32).astype(BF16), earlier.astype(F32).astype(BF16), preferred_element_type=F32)
    place = jnp.sum(jnp.where(named, before, 0.0), axis=0, keepdims=True)
    return labels * capacity + place.astype(jnp.int32)


def slot_table(slots, count):
    table = lax.broadcasted_iota(jnp.int32, (count, slots.shape[1]), 0) == slots
    return table.astype(F32).astype(BF16)


def pack_kernel(experts, capacity, ids_hbm, rows_hbm, grad_hbm, out, slots, ids, rows, grad, sems):
    copies = [
        pltpu.make_async_copy(src, dst, sems.at[i])
        for i, (src, dst) in enumerate(((ids_hbm, ids), (rows_hbm, rows), (grad_hbm, grad)))
    ]
    for copy in copies:
        copy.start()
    copies[0].wait()
    slots[...] = slots_of(ids[...], experts, capacity)
    table = slot_table(slots[...], experts * capacity)
    width = rows.shape[1]
    for i, ref in enumerate((rows, grad)):
        copies[1 + i].wait()
        out[:, pl.ds(i * width, width)] = jnp.dot(table, ref[...], preferred_element_type=F32).astype(BF16)


def pack(ids, rows, grad, experts, capacity):
    shape = (experts * capacity, 2 * rows.shape[1])
    ids, rows, grad = (pltpu.with_memory_space_constraint(x, pltpu.HBM) for x in (ids, rows, grad))
    return pl.pallas_call(
        functools.partial(pack_kernel, experts, capacity),
        out_shape=(jax.ShapeDtypeStruct(shape, BF16), jax.ShapeDtypeStruct(ids.shape, ids.dtype)),
        in_specs=[HBM] * 3,
        out_specs=(VMEM, VMEM),
        scratch_shapes=[
            pltpu.VMEM(ids.shape, ids.dtype),
            pltpu.VMEM(rows.shape, rows.dtype),
            pltpu.VMEM(grad.shape, grad.dtype),
            DMA((3,)),
        ],
        compiler_params=limit(4),
        name="pack",
    )(ids, rows, grad)


def unpack_kernel(experts, replicas, capacity, slots_ref, parts_ref, out_ref):
    table = slot_table(slots_ref[...], experts * capacity)
    total = parts_ref[:, 0].astype(F32)
    for replica in range(1, replicas):
        total = total + parts_ref[:, replica].astype(F32)
    total = total.astype(BF16).reshape(experts * capacity, out_ref.shape[1])
    out_ref[...] = lax.dot_general(
        table, total, (((0,), (0,)), ((), ())), preferred_element_type=F32
    ).astype(BF16)


def unpack(slots, parts, experts, replicas, capacity):
    return pl.pallas_call(
        functools.partial(unpack_kernel, experts, replicas, capacity),
        out_shape=jax.ShapeDtypeStruct((slots.shape[1], parts.shape[-1]), BF16),
        in_specs=[VMEM] * 2,
        out_specs=VMEM,
        compiler_params=limit(8),
        name="unpack",
    )(slots, parts)


def group_math(pieces, win_ref, wout_ref, keep):
    width = win_ref.shape[0]
    hidden = win_ref.shape[1]
    tile = 256
    both = jnp.concatenate([piece[...] for piece in pieces], axis=0)
    rows_in, rows_grad = both[:, :width], both[:, width:]
    total = None
    for at in range(0, hidden, tile):
        win = win_ref[:, at : at + tile]
        preact = jnp.dot(rows_in, win, preferred_element_type=F32)
        grad_act = lax.dot_general(
            rows_grad, wout_ref[at : at + tile, :], (((1,), (1,)), ((), ())), preferred_element_type=F32
        )
        gate_sig = jax.nn.sigmoid(preact)
        grad_pre = (grad_act * gate_sig * (1.0 + preact * (1.0 - gate_sig))).astype(BF16)
        if keep is not None:
            keep(at, tile, (preact * gate_sig).astype(BF16), grad_pre)
        part = lax.dot_general(grad_pre, win, (((1,), (1,)), ((), ())), preferred_element_type=F32)
        total = part if total is None else total + part
    return total.astype(BF16)


def keep_rows(pieces, rows_hbm, sems):
    copies = []
    at = 0
    for piece in pieces:
        rows = pl.ds(at, piece.shape[0])
        at += piece.shape[0]
        copies.append(pltpu.make_async_copy(piece, rows_hbm.at[rows], sems.at[len(copies)]))
        copies[-1].start()
    return copies


def group_kernel(count, *refs):
    win_ref, wout_ref, act_hbm, pre_hbm, rows_hbm, part_ref, act_ref, pre_ref, sems, rows_sems = refs[count:]
    copies = keep_rows(refs[:count], rows_hbm, rows_sems)
    others = len(copies)

    def keep(at, tile, *values):
        columns = pl.ds(at, tile)
        for value, ref, hbm in zip(values, (act_ref, pre_ref), (act_hbm, pre_hbm)):
            ref[:, columns] = value
            copies.append(pltpu.make_async_copy(ref.at[:, columns], hbm.at[:, columns], sems.at[len(copies) - others]))
            copies[-1].start()

    part_ref[...] = group_math(refs[:count], win_ref, wout_ref, keep).reshape(part_ref.shape)
    for copy in copies:
        copy.wait()


def last_kernel(count, where_ref, *refs):
    win_ref, wout_ref, own_ref, near_ref, late_ref, out_hbm, rows_hbm, part, sems, rows_sems = refs[count:]
    sources, replicas = out_hbm.shape[:2]
    cut = sources // 2
    at = [lax.rem(where_ref[0] + k, replicas) for k in range(replicas)]
    copies = []

    def put(ref, low, high):
        for first, replica in ((0, low), (cut, high)):
            rows = pl.ds(first, cut)
            copies.append(pltpu.make_async_copy(ref.at[rows], out_hbm.at[rows, replica], sems.at[len(copies)]))
            copies[-1].start()

    put(own_ref, at[0], at[0])
    put(near_ref, at[3], at[1])
    put(late_ref, at[1], at[3])
    kept = keep_rows(refs[:count], rows_hbm, rows_sems)
    part[...] = group_math(refs[:count], win_ref, wout_ref, None).reshape(part.shape)
    put(part, at[2], at[2])
    for copy in copies + kept:
        copy.wait()


def cost(rows, width, hidden):
    return pl.CostEstimate(
        flops=6 * rows * width * hidden, bytes_accessed=4 * width * hidden, transcendentals=rows * hidden
    )


def group(pieces, win, wout, capacity):
    rows = sum(piece.shape[0] for piece in pieces)
    width, hidden = win.shape
    return pl.pallas_call(
        functools.partial(group_kernel, len(pieces)),
        out_shape=(
            pltpu.HBM((rows, hidden), BF16),
            pltpu.HBM((rows, hidden), BF16),
            pltpu.HBM((rows, 2 * width), BF16),
            jax.ShapeDtypeStruct((rows // capacity, capacity, width), BF16),
        ),
        in_specs=[VMEM] * (len(pieces) + 2),
        out_specs=(HBM, HBM, HBM, VMEM),
        scratch_shapes=[
            pltpu.VMEM((rows, hidden), BF16),
            pltpu.VMEM((rows, hidden), BF16),
            DMA((8,)),
            DMA((len(pieces),)),
        ],
        compiler_params=limit(16),
        cost_estimate=cost(rows, width, hidden),
        name="group",
    )(*pieces, win, wout)


def last_group(where, pieces, win, wout, own, near, late, replicas):
    rows = sum(piece.shape[0] for piece in pieces)
    width, hidden = win.shape
    sources, capacity = own.shape[:2]
    return pl.pallas_call(
        functools.partial(last_kernel, len(pieces)),
        out_shape=(
            pltpu.HBM((sources, replicas, capacity, width), BF16),
            pltpu.HBM((rows, 2 * width), BF16),
        ),
        in_specs=[SMEM] + [VMEM] * (len(pieces) + 5),
        out_specs=(HBM, HBM),
        scratch_shapes=[pltpu.VMEM(own.shape, BF16), DMA((8,)), DMA((len(pieces),))],
        compiler_params=limit(16),
        cost_estimate=cost(rows, width, hidden),
        name="last_group",
    )(where, *pieces, win, wout, own, near, late)


def again_kernel(rows_ref, win_ref, wout_ref, act_ref, pre_ref):
    width = win_ref.shape[0]
    rows = rows_ref[...]
    preact = jnp.dot(rows[:, :width], win_ref[...], preferred_element_type=F32)
    grad_act = lax.dot_general(rows[:, width:], wout_ref[...], (((1,), (1,)), ((), ())), preferred_element_type=F32)
    gate_sig = jax.nn.sigmoid(preact)
    act_ref[...] = (preact * gate_sig).astype(BF16)
    pre_ref[...] = (grad_act * gate_sig * (1.0 + preact * (1.0 - gate_sig))).astype(BF16)


def again(rows, win, wout):
    width, hidden = win.shape
    tile = 256
    out = jax.ShapeDtypeStruct((rows.shape[0], hidden), BF16)
    return pl.pallas_call(
        again_kernel,
        out_shape=(out, out),
        grid=(hidden // tile,),
        in_specs=[
            VMEM,
            pl.BlockSpec((width, tile), lambda j: (0, j)),
            pl.BlockSpec((tile, width), lambda j: (j, 0)),
        ],
        out_specs=(pl.BlockSpec((rows.shape[0], tile), lambda j: (0, j)),) * 2,
        cost_estimate=pl.CostEstimate(
            flops=4 * rows.shape[0] * width * hidden,
            bytes_accessed=4 * width * hidden,
            transcendentals=rows.shape[0] * hidden,
        ),
        name="again",
    )(rows, win, wout)


def weights_kernel(pieces, groups, *refs):
    rows_refs, act_refs, pre_refs = refs[:pieces], refs[pieces : pieces + groups], refs[pieces + groups : pieces + 2 * groups]
    first_ref, second_ref, turned = refs[pieces + 2 * groups :]
    width, _ = first_ref.shape

    @pl.when(pl.program_id(0) == 0)
    def _():
        rows = jnp.concatenate([ref[:, :width] for ref in rows_refs], axis=0)
        turned[...] = rows.T

    pre = jnp.concatenate([ref[...] for ref in pre_refs], axis=0)
    first_ref[...] = jnp.dot(turned[...], pre, preferred_element_type=F32)
    act = jnp.concatenate([ref[...] for ref in act_refs], axis=0)
    grad = jnp.concatenate([ref[:, width:] for ref in rows_refs], axis=0)
    second_ref[...] = lax.dot_general(act, grad, (((0,), (0,)), ((), ())), preferred_element_type=F32)


def weight_grads(pieces, acts, pres, width):
    rows = sum(piece.shape[0] for piece in pieces)
    hidden = acts[0].shape[1]
    tile = 256
    return pl.pallas_call(
        functools.partial(weights_kernel, len(pieces), len(acts)),
        out_shape=(
            jax.ShapeDtypeStruct((width, hidden), F32),
            jax.ShapeDtypeStruct((hidden, width), F32),
        ),
        grid=(hidden // tile,),
        in_specs=[VMEM] * len(pieces) + [pl.BlockSpec((act.shape[0], tile), lambda j: (0, j)) for act in acts + pres],
        out_specs=(pl.BlockSpec((width, tile), lambda j: (0, j)), pl.BlockSpec((tile, width), lambda j: (j, 0))),
        scratch_shapes=[pltpu.VMEM((width, rows), BF16)],
        cost_estimate=pl.CostEstimate(
            flops=4 * rows * width * hidden, bytes_accessed=8 * width * hidden, transcendentals=0
        ),
        name="weights",
    )(*pieces, *acts, *pres)


def steps(atom_rows, grad_out, expert_ids, weight_in, weight_out):
    experts = lax.axis_size("expert")
    replicas = lax.axis_size("replica")
    local_rows = atom_rows.shape[0]
    width = atom_rows.shape[1]
    capacity = 2 * local_rows // experts
    win, wout = weight_in[0], weight_out[0]
    ids = expert_ids.reshape(1, local_rows)
    where = lax.axis_index("replica").astype(jnp.int32).reshape(1)
    packed, slots = pack(ids, atom_rows, grad_out, experts, capacity)
    own = lax.all_to_all(
        packed.reshape(experts, capacity, 2 * width), "expert", split_axis=0, concat_axis=0, tiled=True
    ).reshape(experts * capacity, 2 * width)
    up = [(i, (i + 1) % replicas) for i in range(replicas)]
    down = [(i, (i - 1) % replicas) for i in range(replicas)]
    half = experts * capacity // 2
    low, high = own[:half], own[half:]

    def send(rows, way):
        return lax.ppermute(rows, "replica", way)

    below_low = send(low, up)
    above_high = send(high, down)
    below_high = send(high, up)
    above_low = send(low, down)
    far_low = send(below_low, up)
    far_high = send(above_high, down)
    act0, pre0, rows0, part0 = group([low, high], win, wout, capacity)
    act1, pre1, rows1, part1 = group([below_low, above_high], win, wout, capacity)
    act2, pre2, rows2, part2 = group([above_low, below_high], win, wout, capacity)
    sending, rows3 = last_group(where, [far_low, far_high], win, wout, part0, part1, part2, replicas)
    returned = lax.all_to_all(
        sending.reshape(experts * replicas, capacity, width),
        ("expert", "replica"),
        split_axis=0,
        concat_axis=0,
        tiled=True,
    )
    act3, pre3 = again(rows3, weight_in[0], weight_out[0])
    grad_first, grad_second = weight_grads(
        [rows0, rows1, rows2, rows3],
        [act0, act1, act2, act3],
        [pre0, pre1, pre2, pre3],
        width,
    )
    grad_rows = unpack(slots, returned.reshape(experts, replicas, capacity, width), experts, replicas, capacity)
    return (grad_rows, grad_first[None], grad_second[None])


def solution(mesh):
    rows = P(("expert", "replica"), None)
    first = P("expert", None, "replica")
    second = P("expert", "replica", None)
    return jax.shard_map(
        steps,
        mesh=mesh,
        in_specs=(rows, rows, rows, first, second),
        out_specs=(rows, first, second),
        check_vma=False,
    )
```

```python
import functools

import jax
import jax.numpy as jnp
from jax import lax
from jax.experimental import pallas as pl
from jax.experimental.pallas import tpu as pltpu
from jax.sharding import PartitionSpec as P


VMEM = pl.BlockSpec(memory_space=pltpu.VMEM)
SMEM = pl.BlockSpec(memory_space=pltpu.SMEM)
HBM = pl.BlockSpec(memory_space=pltpu.HBM)
DMA = pltpu.SemaphoreType.DMA
BF16 = jnp.bfloat16
F32 = jnp.float32


def limit(mib):
    return pltpu.CompilerParams(vmem_limit_bytes=mib << 20)


def slots_of(labels, experts, capacity):
    rows = labels.shape[1]
    named = lax.broadcasted_iota(jnp.int32, (experts, rows), 0) == labels
    earlier = lax.broadcasted_iota(jnp.int32, (rows, rows), 0) < lax.broadcasted_iota(jnp.int32, (rows, rows), 1)
    before = jnp.dot(named.astype(F32).astype(BF16), earlier.astype(F32).astype(BF16), preferred_element_type=F32)
    place = jnp.sum(jnp.where(named, before, 0.0), axis=0, keepdims=True)
    return labels * capacity + place.astype(jnp.int32)


def slot_table(slots, count):
    table = lax.broadcasted_iota(jnp.int32, (count, slots.shape[1]), 0) == slots
    return table.astype(F32).astype(BF16)


def pack_kernel(experts, capacity, ids_hbm, rows_hbm, grad_hbm, out, slots, ids, rows, grad, sems):
    copies = [
        pltpu.make_async_copy(src, dst, sems.at[i])
        for i, (src, dst) in enumerate(((ids_hbm, ids), (rows_hbm, rows), (grad_hbm, grad)))
    ]
    for copy in copies:
        copy.start()
    copies[0].wait()
    slots[...] = slots_of(ids[...], experts, capacity)
    table = slot_table(slots[...], experts * capacity)
    width = rows.shape[1]
    for i, ref in enumerate((rows, grad)):
        copies[1 + i].wait()
        out[:, pl.ds(i * width, width)] = jnp.dot(table, ref[...], preferred_element_type=F32).astype(BF16)


def pack(ids, rows, grad, experts, capacity):
    shape = (experts * capacity, 2 * rows.shape[1])
    ids, rows, grad = (pltpu.with_memory_space_constraint(x, pltpu.HBM) for x in (ids, rows, grad))
    return pl.pallas_call(
        functools.partial(pack_kernel, experts, capacity),
        out_shape=(jax.ShapeDtypeStruct(shape, BF16), jax.ShapeDtypeStruct(ids.shape, ids.dtype)),
        in_specs=[HBM] * 3,
        out_specs=(VMEM, VMEM),
        scratch_shapes=[
            pltpu.VMEM(ids.shape, ids.dtype),
            pltpu.VMEM(rows.shape, rows.dtype),
            pltpu.VMEM(grad.shape, grad.dtype),
            DMA((3,)),
        ],
        compiler_params=limit(4),
        name="pack",
    )(ids, rows, grad)


def unpack_kernel(experts, replicas, capacity, slots_ref, parts_ref, out_ref):
    table = slot_table(slots_ref[...], experts * capacity)
    total = parts_ref[:, 0].astype(F32)
    for replica in range(1, replicas):
        total = total + parts_ref[:, replica].astype(F32)
    total = total.astype(BF16).reshape(experts * capacity, out_ref.shape[1])
    out_ref[...] = lax.dot_general(
        table, total, (((0,), (0,)), ((), ())), preferred_element_type=F32
    ).astype(BF16)


def unpack(slots, parts, experts, replicas, capacity):
    return pl.pallas_call(
        functools.partial(unpack_kernel, experts, replicas, capacity),
        out_shape=jax.ShapeDtypeStruct((slots.shape[1], parts.shape[-1]), BF16),
        in_specs=[VMEM] * 2,
        out_specs=VMEM,
        compiler_params=limit(8),
        name="unpack",
    )(slots, parts)


def group_math(pieces, win_ref, wout_ref, keep):
    width = win_ref.shape[0]
    hidden = win_ref.shape[1]
    tile = 256
    both = jnp.concatenate([piece[...] for piece in pieces], axis=0)
    rows_in, rows_grad = both[:, :width], both[:, width:]
    total = None
    for at in range(0, hidden, tile):
        win = win_ref[:, at : at + tile]
        preact = jnp.dot(rows_in, win, preferred_element_type=F32)
        grad_act = lax.dot_general(
            rows_grad, wout_ref[at : at + tile, :], (((1,), (1,)), ((), ())), preferred_element_type=F32
        )
        gate_sig = jax.nn.sigmoid(preact)
        grad_pre = (grad_act * gate_sig * (1.0 + preact * (1.0 - gate_sig))).astype(BF16)
        if keep is not None:
            keep(at, tile, (preact * gate_sig).astype(BF16), grad_pre)
        part = lax.dot_general(grad_pre, win, (((1,), (1,)), ((), ())), preferred_element_type=F32)
        total = part if total is None else total + part
    return total.astype(BF16)


def keep_rows(pieces, rows_hbm, sems):
    copies = []
    at = 0
    for piece in pieces:
        rows = pl.ds(at, piece.shape[0])
        at += piece.shape[0]
        copies.append(pltpu.make_async_copy(piece, rows_hbm.at[rows], sems.at[len(copies)]))
        copies[-1].start()
    return copies


def group_kernel(count, *refs):
    win_ref, wout_ref, act_hbm, pre_hbm, rows_hbm, part_ref, act_ref, pre_ref, sems, rows_sems = refs[count:]
    copies = keep_rows(refs[:count], rows_hbm, rows_sems)
    others = len(copies)

    def keep(at, tile, *values):
        columns = pl.ds(at, tile)
        for value, ref, hbm in zip(values, (act_ref, pre_ref), (act_hbm, pre_hbm)):
            ref[:, columns] = value
            copies.append(pltpu.make_async_copy(ref.at[:, columns], hbm.at[:, columns], sems.at[len(copies) - others]))
            copies[-1].start()

    part_ref[...] = group_math(refs[:count], win_ref, wout_ref, keep).reshape(part_ref.shape)
    for copy in copies:
        copy.wait()


def last_kernel(count, cut, where_ref, *refs):
    win_ref, wout_ref, own_ref, near_ref, late_ref, out_hbm, rows_hbm, part, sems, rows_sems = refs[count:]
    sources, replicas = out_hbm.shape[:2]
    at = [lax.rem(where_ref[0] + k, replicas) for k in range(replicas)]
    copies = []

    def put(ref, low, high):
        for first, some, replica in ((0, cut, low), (cut, sources - cut, high)):
            rows = pl.ds(first, some)
            copies.append(pltpu.make_async_copy(ref.at[rows], out_hbm.at[rows, replica], sems.at[len(copies)]))
            copies[-1].start()

    put(own_ref, at[0], at[0])
    put(near_ref, at[3], at[1])
    put(late_ref, at[1], at[3])
    kept = keep_rows(refs[:count], rows_hbm, rows_sems)
    part[...] = group_math(refs[:count], win_ref, wout_ref, None).reshape(part.shape)
    put(part, at[2], at[2])
    for copy in copies + kept:
        copy.wait()


def cost(rows, width, hidden):
    return pl.CostEstimate(
        flops=6 * rows * width * hidden, bytes_accessed=4 * width * hidden, transcendentals=rows * hidden
    )


def group(pieces, win, wout, capacity):
    rows = sum(piece.shape[0] for piece in pieces)
    width, hidden = win.shape
    return pl.pallas_call(
        functools.partial(group_kernel, len(pieces)),
        out_shape=(
            pltpu.HBM((rows, hidden), BF16),
            pltpu.HBM((rows, hidden), BF16),
            pltpu.HBM((rows, 2 * width), BF16),
            jax.ShapeDtypeStruct((rows // capacity, capacity, width), BF16),
        ),
        in_specs=[VMEM] * (len(pieces) + 2),
        out_specs=(HBM, HBM, HBM, VMEM),
        scratch_shapes=[
            pltpu.VMEM((rows, hidden), BF16),
            pltpu.VMEM((rows, hidden), BF16),
            DMA((8,)),
            DMA((len(pieces),)),
        ],
        compiler_params=limit(16),
        cost_estimate=cost(rows, width, hidden),
        name="group",
    )(*pieces, win, wout)


def last_group(where, pieces, win, wout, own, near, late, replicas):
    rows = sum(piece.shape[0] for piece in pieces)
    width, hidden = win.shape
    sources, capacity = own.shape[:2]
    return pl.pallas_call(
        functools.partial(last_kernel, len(pieces), pieces[0].shape[0] // capacity),
        out_shape=(
            pltpu.HBM((sources, replicas, capacity, width), BF16),
            pltpu.HBM((rows, 2 * width), BF16),
        ),
        in_specs=[SMEM] + [VMEM] * (len(pieces) + 5),
        out_specs=(HBM, HBM),
        scratch_shapes=[pltpu.VMEM(own.shape, BF16), DMA((8,)), DMA((len(pieces),))],
        compiler_params=limit(16),
        cost_estimate=cost(rows, width, hidden),
        name="last_group",
    )(where, *pieces, win, wout, own, near, late)


def again_kernel(rows_ref, win_ref, wout_ref, act_ref, pre_ref):
    width = win_ref.shape[0]
    rows = rows_ref[...]
    preact = jnp.dot(rows[:, :width], win_ref[...], preferred_element_type=F32)
    grad_act = lax.dot_general(rows[:, width:], wout_ref[...], (((1,), (1,)), ((), ())), preferred_element_type=F32)
    gate_sig = jax.nn.sigmoid(preact)
    act_ref[...] = (preact * gate_sig).astype(BF16)
    pre_ref[...] = (grad_act * gate_sig * (1.0 + preact * (1.0 - gate_sig))).astype(BF16)


def again(rows, win, wout):
    width, hidden = win.shape
    tile = 256
    out = jax.ShapeDtypeStruct((rows.shape[0], hidden), BF16)
    return pl.pallas_call(
        again_kernel,
        out_shape=(out, out),
        grid=(hidden // tile,),
        in_specs=[
            VMEM,
            pl.BlockSpec((width, tile), lambda j: (0, j)),
            pl.BlockSpec((tile, width), lambda j: (j, 0)),
        ],
        out_specs=(pl.BlockSpec((rows.shape[0], tile), lambda j: (0, j)),) * 2,
        cost_estimate=pl.CostEstimate(
            flops=4 * rows.shape[0] * width * hidden,
            bytes_accessed=4 * width * hidden,
            transcendentals=rows.shape[0] * hidden,
        ),
        name="again",
    )(rows, win, wout)


def weights_kernel(pieces, groups, *refs):
    rows_refs, act_refs, pre_refs = refs[:pieces], refs[pieces : pieces + groups], refs[pieces + groups : pieces + 2 * groups]
    first_ref, second_ref, turned = refs[pieces + 2 * groups :]
    width, _ = first_ref.shape

    @pl.when(pl.program_id(0) == 0)
    def _():
        rows = jnp.concatenate([ref[:, :width] for ref in rows_refs], axis=0)
        turned[...] = rows.T

    pre = jnp.concatenate([ref[...] for ref in pre_refs], axis=0)
    first_ref[...] = jnp.dot(turned[...], pre, preferred_element_type=F32)
    act = jnp.concatenate([ref[...] for ref in act_refs], axis=0)
    grad = jnp.concatenate([ref[:, width:] for ref in rows_refs], axis=0)
    second_ref[...] = lax.dot_general(act, grad, (((0,), (0,)), ((), ())), preferred_element_type=F32)


def weight_grads(pieces, acts, pres, width):
    rows = sum(piece.shape[0] for piece in pieces)
    hidden = acts[0].shape[1]
    tile = 256
    return pl.pallas_call(
        functools.partial(weights_kernel, len(pieces), len(acts)),
        out_shape=(
            jax.ShapeDtypeStruct((width, hidden), F32),
            jax.ShapeDtypeStruct((hidden, width), F32),
        ),
        grid=(hidden // tile,),
        in_specs=[VMEM] * len(pieces) + [pl.BlockSpec((act.shape[0], tile), lambda j: (0, j)) for act in acts + pres],
        out_specs=(pl.BlockSpec((width, tile), lambda j: (0, j)), pl.BlockSpec((tile, width), lambda j: (j, 0))),
        scratch_shapes=[pltpu.VMEM((width, rows), BF16)],
        cost_estimate=pl.CostEstimate(
            flops=4 * rows * width * hidden, bytes_accessed=8 * width * hidden, transcendentals=0
        ),
        name="weights",
    )(*pieces, *acts, *pres)


def steps(atom_rows, grad_out, expert_ids, weight_in, weight_out):
    experts = lax.axis_size("expert")
    replicas = lax.axis_size("replica")
    local_rows = atom_rows.shape[0]
    width = atom_rows.shape[1]
    capacity = 2 * local_rows // experts
    win, wout = weight_in[0], weight_out[0]
    ids = expert_ids.reshape(1, local_rows)
    where = lax.axis_index("replica").astype(jnp.int32).reshape(1)
    packed, slots = pack(ids, atom_rows, grad_out, experts, capacity)
    own = lax.all_to_all(
        packed.reshape(experts, capacity, 2 * width), "expert", split_axis=0, concat_axis=0, tiled=True
    ).reshape(experts * capacity, 2 * width)
    up = [(i, (i + 1) % replicas) for i in range(replicas)]
    down = [(i, (i - 1) % replicas) for i in range(replicas)]
    half = 9 * experts * capacity // 16
    low, high = own[:half], own[half:]

    def send(rows, way):
        return lax.ppermute(rows, "replica", way)

    below_low = send(low, up)
    above_high = send(high, down)
    below_high = send(high, up)
    above_low = send(low, down)
    far_low = send(below_low, up)
    far_high = send(above_high, down)
    act0, pre0, rows0, part0 = group([low, high], win, wout, capacity)
    act1, pre1, rows1, part1 = group([below_low, above_high], win, wout, capacity)
    act2, pre2, rows2, part2 = group([above_low, below_high], win, wout, capacity)
    sending, rows3 = last_group(where, [far_low, far_high], win, wout, part0, part1, part2, replicas)
    returned = lax.all_to_all(
        sending.reshape(experts * replicas, capacity, width),
        ("expert", "replica"),
        split_axis=0,
        concat_axis=0,
        tiled=True,
    )
    act3, pre3 = again(rows3, weight_in[0], weight_out[0])
    grad_first, grad_second = weight_grads(
        [rows0, rows1, rows2, rows3],
        [act0, act1, act2, act3],
        [pre0, pre1, pre2, pre3],
        width,
    )
    grad_rows = unpack(slots, returned.reshape(experts, replicas, capacity, width), experts, replicas, capacity)
    return (grad_rows, grad_first[None], grad_second[None])


def solution(mesh):
    rows = P(("expert", "replica"), None)
    first = P("expert", None, "replica")
    second = P("expert", "replica", None)
    return jax.shard_map(
        steps,
        mesh=mesh,
        in_specs=(rows, rows, rows, first, second),
        out_specs=(rows, first, second),
        check_vma=False,
    )
```
